32 devices in a mesh: section: 4 (over z), tensor: 8 (over y, x, core).
Axes of the slice: x: 2, y: 2, z: 4, core: 2. Of those that a mesh axis runs over, the one named last changes fastest.
Arguments:
- activations: bfloat16 [4, 8192, 128], P('section', 'tensor'), may hold values from -6 to 6
- out_grads: bfloat16 [4, 8192, 128], P('section', 'tensor'), may hold values from -1.5 to 1.5
- w_in: bfloat16 [4, 256, 6, 128, 128], P('section', 'tensor'), may hold values from -0.25 to 0.25
- w_out: bfloat16 [4, 256, 6, 128, 128], P('section', 'tensor'), may hold values from -0.25 to 0.25
- bias_in: bfloat16 [4, 32768], P('section', 'tensor'), may hold values from -3 to 3
- cols_in: int32 [4, 256, 6], P('section', 'tensor'), may hold values from 0 to 63, as said below
- mask_in: int32 [4, 256, 6], P('section', 'tensor'), may hold values from 0 to 1, as said below
- cols_out: int32 [4, 256, 6], P('section', 'tensor'), may hold values from 0 to 63, as said below
- mask_out: int32 [4, 256, 6], P('section', 'tensor'), may hold values from 0 to 1, as said below
- block_rows: int32 [4, 256], P('section', 'tensor'), may hold values from 0 to 255, each once within a row
Outputs:
- grad_w_in: bfloat16 [4, 256, 6, 128, 128], P('section', 'tensor')
- grad_w_out: bfloat16 [4, 256, 6, 128, 128], P('section', 'tensor')
- grad_bias: float32 [4, 32768], P('section', 'tensor')
- handed: bfloat16 [4, 8192, 128], P('section', 'tensor')
The draws below stay inside these ranges and needn't reach their ends.
Inputs may be any that keep to these rules, and one draw needn't show every extreme that they name: `cols_in`: in each stored row the 6 entries are distinct feature blocks; only slots with mask_in 1 are used. `mask_in`: each stored row has its valid slots first: 1 on the first 2 to 6 slots, 0 after; some row of every draw has all 6 slots valid. `cols_out`: in each stored row the 6 entries are distinct feature blocks; only slots with mask_out 1 are used. `mask_out`: each stored row has its valid slots first: 1 on the first 2 to 6 slots, 0 after; some row of every draw has all 6 slots valid. `block_rows`: for each section, a permutation of the 256 hidden blocks.
All inputs are finite; a program needn't handle non-finite values.
Results may differ from the reference program's by a relative error of at most 0.0049.
Values may be sent and summed in bfloat16 or wider, within the bound.
A program may use at most 128 MiB of HBM per device.

```python
import jax
import jax.numpy as jnp
from jax import lax

D = 8192
FF = 32768
BLK = 128
S = 6
TOK = 128
SECTIONS = 4
DBLOCKS = 64
HBLOCKS = 256


def pattern_draw(key, salt):
    key = jax.random.fold_in(key, salt)
    key_order, key_base, key_extra, key_gate, key_full = jax.random.split(key, 5)
    total = SECTIONS * HBLOCKS
    scores = jax.random.randint(key_order, (total, DBLOCKS), 0, 1 << 20) * DBLOCKS + jnp.arange(DBLOCKS, dtype=jnp.int32)[None, :]
    order = jnp.argsort(scores, axis=1)[:, :S].astype(jnp.int32)
    base = jax.random.randint(key_base, (total,), 0, 5)
    extra = jax.random.randint(key_extra, (total,), 0, S - 5)
    gate = jax.random.randint(key_gate, (total,), 0, 4) == 0
    count = jnp.minimum(2 + base + jnp.where(gate, extra, 0), S)
    full_row = jax.random.randint(key_full, (), 0, total)
    count = jnp.where(jnp.arange(total, dtype=jnp.int32) == full_row, S, count)
    valid = (jnp.arange(S, dtype=jnp.int32)[None, :] < count[:, None]).astype(jnp.int32)
    return (order.reshape(SECTIONS, HBLOCKS, S), valid.reshape(SECTIONS, HBLOCKS, S))


def draw_cols_in(key, part):
    return pattern_draw(key, 11)[0]


def draw_mask_in(key, part):
    return pattern_draw(key, 11)[1]


def draw_cols_out(key, part):
    return pattern_draw(key, 23)[0]


def draw_mask_out(key, part):
    return pattern_draw(key, 23)[1]


def level_of(rng, shape, cuts, low, high):
    level, own = 1.0, jax.random.fold_in(rng, 6)
    for position, shards_of in cuts:
        heights = jnp.exp(jax.random.uniform(jax.random.fold_in(own, position), (shards_of,), jnp.float32, low / len(cuts), high / len(cuts)))
        level = level * jnp.repeat(heights, shape[position] // shards_of).reshape([-1 if axis == position else 1 for axis in range(len(shape))])
    return level


def noise(key, shape, width, limit, shards=(), kind=jnp.bfloat16):
    values = width * jax.random.normal(key, shape, jnp.float32)
    if shards:
        values = values * level_of(key, shape, shards, -0.22, 0.18)
    return jnp.clip(values, -limit, limit).astype(kind)


def setup_inputs(seed: int = 0) -> dict:
    arg_keys = jax.random.split(jax.random.key(seed), 11)
    activations = noise(arg_keys[0], (SECTIONS, D, TOK), 1.0, 6.0, ((0, 4), (1, 8)))
    out_grads = noise(arg_keys[1], (SECTIONS, D, TOK), 0.25, 1.5, ((0, 4), (1, 8)))
    w_in = noise(arg_keys[2], (SECTIONS, HBLOCKS, S, BLK, BLK), (4 * BLK) ** -0.5, 0.25, ((0, 4), (1, 8)))
    w_out = noise(arg_keys[3], (SECTIONS, HBLOCKS, S, BLK, BLK), (4 * BLK) ** -0.5, 0.25, ((0, 4), (1, 8)))
    bias_in = noise(arg_keys[4], (SECTIONS, FF), 0.5, 3.0, ((0, 4), (1, 8)))
    cols_in = draw_cols_in(jax.random.fold_in(arg_keys[10], 71), 0)
    mask_in = draw_mask_in(jax.random.fold_in(arg_keys[10], 71), 0)
    cols_out = draw_cols_out(jax.random.fold_in(arg_keys[10], 71), 0)
    mask_out = draw_mask_out(jax.random.fold_in(arg_keys[10], 71), 0)
    block_rows = jax.vmap(lambda own: jax.random.permutation(own, HBLOCKS))(jax.random.split(arg_keys[9], SECTIONS)).reshape((SECTIONS, HBLOCKS)).astype(jnp.int32)
    return dict(activations=activations, out_grads=out_grads, w_in=w_in, w_out=w_out, bias_in=bias_in, cols_in=cols_in, mask_in=mask_in, cols_out=cols_out, mask_out=mask_out, block_rows=block_rows)


def gelu_parts(pre_act):
    cdf_part = 0.5 * (1.0 + jax.scipy.special.erf(pre_act * 0.7071067811865476))
    density = jnp.exp(-0.5 * pre_act * pre_act) * 0.3989422804014327
    return pre_act * cdf_part, cdf_part + pre_act * density


def section_backward(activ, grads, w_in, w_out, bias_in, cols_in, mask_in, cols_out, mask_out, block_rows):
    act_blocks = activ.reshape(DBLOCKS, BLK, TOK).astype(jnp.float32)
    grad_blocks = grads.reshape(DBLOCKS, BLK, TOK).astype(jnp.float32)
    bias_blocks = bias_in.reshape(HBLOCKS, BLK).astype(jnp.float32)
    group_rows = 16
    groups = HBLOCKS // group_rows

    def split(array):
        return array.reshape((groups, group_rows) + array.shape[1:])

    def step(input_grad, item):
        wide_in, wide_out, col_in, valid_in, col_out, valid_out, stored = item
        keep_in = (valid_in > 0)[:, :, None, None]
        keep_out = (valid_out > 0)[:, :, None, None]
        w_in_f = jnp.where(keep_in, wide_in.astype(jnp.float32), 0.0)
        w_out_f = jnp.where(keep_out, wide_out.astype(jnp.float32), 0.0)
        slots_act = act_blocks[col_in]
        slots_grad = grad_blocks[col_out]
        pre_act = jnp.einsum('rsij,rsjt->rit', w_in_f, slots_act) + bias_blocks[stored][:, :, None]
        act_value, gelu_slope = gelu_parts(pre_act)
        hidden = lax.optimization_barrier(act_value.astype(jnp.bfloat16)).astype(jnp.float32)
        grad_hidden = jnp.einsum('rsij,rsjt->rit', w_out_f, slots_grad)
        grad_pre = grad_hidden * gelu_slope
        grad_low = lax.optimization_barrier(grad_pre.astype(jnp.bfloat16)).astype(jnp.float32)
        grad_w_out = jnp.where(keep_out, jnp.einsum('rit,rsjt->rsij', hidden, slots_grad), 0.0).astype(jnp.bfloat16)
        grad_w_in = jnp.where(keep_in, jnp.einsum('rit,rsjt->rsij', grad_low, slots_act), 0.0).astype(jnp.bfloat16)
        pieces = jnp.einsum('rsij,rit->rsjt', w_in_f, grad_low)
        input_grad = input_grad.at[col_in.reshape(-1)].add(pieces.reshape(-1, BLK, TOK))
        bias_grad = jnp.sum(grad_pre, axis=2)
        return input_grad, (grad_w_in, grad_w_out, bias_grad)

    start = jnp.zeros((DBLOCKS, BLK, TOK), jnp.float32)
    items = (split(w_in), split(w_out), split(cols_in), split(mask_in), split(cols_out), split(mask_out), split(block_rows))
    input_grad, outputs = lax.scan(step, start, items)
    grad_w_in, grad_w_out, bias_grad = outputs
    bias_full = jnp.zeros((HBLOCKS, BLK), jnp.float32).at[block_rows].set(bias_grad.reshape(HBLOCKS, BLK))
    return (grad_w_in.reshape(HBLOCKS, S, BLK, BLK), grad_w_out.reshape(HBLOCKS, S, BLK, BLK),
            bias_full.reshape(FF), input_grad.reshape(D, TOK))


def reference(activations, out_grads, w_in, w_out, bias_in, cols_in, mask_in, cols_out, mask_out, block_rows):
    list_in = []
    list_out = []
    list_bias = []
    list_input = []
    for section_index in range(SECTIONS):
        result = section_backward(activations[section_index], out_grads[section_index], w_in[section_index],
                                w_out[section_index], bias_in[section_index], cols_in[section_index],
                                mask_in[section_index], cols_out[section_index], mask_out[section_index],
                                block_rows[section_index])
        list_in.append(result[0])
        list_out.append(result[1])
        list_bias.append(result[2])
        list_input.append(result[3])
    handed_list = [list_input[(section_index + 1) % SECTIONS] for section_index in range(SECTIONS)]
    handed = jnp.stack(handed_list).astype(jnp.bfloat16)
    return (jnp.stack(list_in), jnp.stack(list_out), jnp.stack(list_bias), handed)
```

```python
import functools

import jax
import jax.numpy as jnp
from jax import lax
from jax.experimental import pallas as pl
from jax.experimental.pallas import tpu as pltpu
from jax.sharding import PartitionSpec as P

BLK = 128
MESH = pl.DeviceIdType.MESH
BF16 = jnp.bfloat16
F32 = jnp.float32


def gelu_parts(pre_act):
    cdf_part = 0.5 * (1.0 + lax.erf(pre_act * 0.7071067811865476))
    density = jnp.exp(-0.5 * pre_act * pre_act) * 0.3989422804014327
    return (pre_act * cdf_part, cdf_part + pre_act * density)


def gather_kernel(
    tensor, act, grad, bias, act_all, grad_all, bias_all, send, recv, fsend, frecv, own
):
    chips = tensor // 2
    me = lax.axis_index("tensor")
    sec = lax.axis_index("section")
    core = lax.rem(me, 2)
    chip = me // 2
    partner = chip * 2 + (1 - core)
    sources = (act, grad, bias)
    results = (act_all, grad_all, bias_all)

    def other(step):
        return lax.rem(chip + step, chips) * 2 + core

    def behind(step):
        return lax.rem(chip + chips - step, chips) * 2 + core

    barrier = pltpu.get_barrier_semaphore()
    for peer in [partner] + [other(step) for step in range(1, chips)]:
        pl.semaphore_signal(barrier, inc=1, device_id=(sec, peer), device_id_type=MESH)
    pl.semaphore_wait(barrier, chips)

    def far(kind, step):
        return pltpu.make_async_remote_copy(
            src_ref=sources[kind],
            dst_ref=results[kind].at[me],
            send_sem=send.at[kind, step],
            recv_sem=recv.at[kind, step],
            device_id=(sec, other(step)),
            device_id_type=MESH,
        )

    def near(kind, step):
        slot = behind(step)
        return pltpu.make_async_remote_copy(
            src_ref=sources[kind] if step == 0 else results[kind].at[slot],
            dst_ref=results[kind].at[slot],
            send_sem=fsend.at[kind, step],
            recv_sem=frecv.at[kind, step],
            device_id=(sec, partner),
            device_id_type=MESH,
        )

    order = (2, 0, 1)
    for kind in order:
        for step in range(1, chips):
            far(kind, step).start()
    for kind in order:
        near(kind, 0).start()
        pltpu.make_async_copy(sources[kind], results[kind].at[me], own.at[kind]).start()
    for kind in order:
        for step in range(1, chips):
            far(kind, step).wait_recv()
            near(kind, step).start()
    for kind in order:
        pltpu.make_async_copy(sources[kind], results[kind].at[me], own.at[kind]).wait()
        for step in range(1, chips):
            far(kind, step).wait_send()
        for step in range(chips):
            near(kind, step).wait()


def row_kernel(
    slots, rows, dblocks, tensor,
    cols_in, mask_in, cols_out, mask_out, stored,
    w_in, w_out, act, grad, bias,
    hidden_out, low_out, part_out, bias_out,
    total, bias_wide,
):
    row = pl.program_id(0)
    hblocks = rows * tensor

    @pl.when(row == 0)
    def _():
        total[...] = jnp.zeros_like(total)
        bias_out[...] = jnp.zeros_like(bias_out)
        bias_wide[...] = bias[...].reshape(hblocks, BLK).astype(F32)

    def wide(ref):
        return jnp.concatenate([ref[0, s] for s in range(slots)], axis=1)

    def tall(ref, cols, mask):
        return jnp.concatenate(
            [
                jnp.where(mask[row, s] > 0, ref[cols[row, s]], jnp.zeros((BLK, BLK), BF16))
                for s in range(slots)
            ],
            axis=0,
        )

    w_wide = wide(w_in)
    where_row = stored[row]
    bias_row = bias_wide[pl.ds(where_row, 1), :]
    bias_col = jnp.transpose(jnp.broadcast_to(bias_row, (BLK, BLK)))
    pre_act = jnp.dot(w_wide, tall(act, cols_in, mask_in), preferred_element_type=F32) + bias_col
    act_value, slope = gelu_parts(pre_act)
    hidden_out[0] = act_value.astype(BF16)
    grad_hidden = jnp.dot(
        wide(w_out), tall(grad, cols_out, mask_out), preferred_element_type=F32
    )
    grad_pre = grad_hidden * slope
    low_out[0] = grad_pre.astype(BF16)
    turned = jnp.transpose(grad_pre)
    bias_out[pl.ds(where_row, 1), :] = jnp.sum(turned, axis=0, keepdims=True)
    pieces = jnp.dot(turned.astype(BF16), w_wide, preferred_element_type=F32)
    for s in range(slots):

        @pl.when(mask_in[row, s] > 0)
        def _():
            total[cols_in[row, s]] += pieces[:, s * BLK : (s + 1) * BLK]

    @pl.when(row == rows - 1)
    def _():
        chips = tensor // 2
        per = dblocks // tensor
        for chip in range(chips):
            for core in range(2):
                base = (chip * 2 + core) * per
                part_out[core, chip] = total[base : base + per].astype(BF16)


def scatter_kernel(
    tensor, sections, slots, rows, per,
    cols_in, mask_in, cols_out, mask_out,
    part, bias_part, hidden, low, act, grad,
    tiles_in, tiles_out, bias_sum, handed,
    held_in, held_out, from_pair, pair_sum, from_chips, final, bias_from, bias_keep,
    pair_send, pair_recv, chip_send, chip_recv, bias_send, bias_recv, hand_send, hand_recv, store,
):
    chips = tensor // 2
    me = lax.axis_index("tensor")
    sec = lax.axis_index("section")
    core = lax.rem(me, 2)
    chip = me // 2
    partner = chip * 2 + (1 - core)
    before = lax.rem(sec + sections - 1, sections)
    after = lax.rem(sec + 1, sections)

    def ahead_chip(step):
        return lax.rem(chip + step, chips)

    barrier = pltpu.get_barrier_semaphore()
    for step in range(1, tensor):
        pl.semaphore_signal(
            barrier, inc=1, device_id=(sec, lax.rem(me + step, tensor)), device_id_type=MESH
        )
    for section in (before, after):
        pl.semaphore_signal(barrier, inc=1, device_id=(section, me), device_id_type=MESH)
    pl.semaphore_wait(barrier, tensor + 1)

    pair = pltpu.make_async_remote_copy(
        src_ref=part.at[1 - core],
        dst_ref=from_pair,
        send_sem=pair_send,
        recv_sem=pair_recv,
        device_id=(sec, partner),
        device_id_type=MESH,
    )
    pair.start()

    def bias_copy(step):
        peer = lax.rem(me + step, tensor)
        return pltpu.make_async_remote_copy(
            src_ref=bias_part.at[peer],
            dst_ref=bias_from.at[step],
            send_sem=bias_send.at[step],
            recv_sem=bias_recv.at[step],
            device_id=(sec, peer),
            device_id_type=MESH,
        )

    for step in range(1, tensor):
        bias_copy(step).start()

    def chip_copy(step):
        return pltpu.make_async_remote_copy(
            src_ref=pair_sum.at[step],
            dst_ref=from_chips.at[step],
            send_sem=chip_send.at[step],
            recv_sem=chip_recv.at[step],
            device_id=(sec, ahead_chip(step) * 2 + core),
            device_id_type=MESH,
        )

    def tall(ref, cols, mask, row):
        return jnp.concatenate(
            [
                jnp.where(mask[row, s] > 0, ref[cols[row, s]], jnp.zeros((BLK, BLK), BF16))
                for s in range(slots)
            ],
            axis=0,
        )

    def out_product(left, right):
        return lax.dot_general(
            left, right, (((1,), (1,)), ((), ())), preferred_element_type=F32
        ).astype(BF16)

    def one_row(row, carry):
        got_in = out_product(low[row], tall(act, cols_in, mask_in, row))
        got_out = out_product(hidden[row], tall(grad, cols_out, mask_out, row))
        for s in range(slots):
            held_in[row, s] = got_in[:, s * BLK : (s + 1) * BLK]
            held_out[row, s] = got_out[:, s * BLK : (s + 1) * BLK]
        pltpu.make_async_copy(held_in.at[row], tiles_in.at[row], store.at[0]).start()
        pltpu.make_async_copy(held_out.at[row], tiles_out.at[row], store.at[1]).start()
        return carry

    first, second = rows // 4, rows - rows // 4
    lax.fori_loop(0, first, one_row, 0)

    pair.wait()
    for step in list(range(1, chips)) + [0]:
        where_chip = ahead_chip(step)
        pair_sum[step] = (
            part[core, where_chip].astype(F32) + from_pair[where_chip].astype(F32)
        ).astype(BF16)
        if step:
            chip_copy(step).start()

    lax.fori_loop(first, second, one_row, 0)

    result = pair_sum[0].astype(F32)
    for step in range(1, chips):
        chip_copy(step).wait()
        result = result + from_chips[step].astype(F32)
    for block in range(per):
        final[block] = jnp.transpose(result[block]).astype(BF16)
    hand = pltpu.make_async_remote_copy(
        src_ref=final,
        dst_ref=handed,
        send_sem=hand_send,
        recv_sem=hand_recv,
        device_id=(before, me),
        device_id_type=MESH,
    )
    hand.start()

    lax.fori_loop(second, rows, one_row, 0)

    bias_total = bias_part[me]
    for step in range(1, tensor):
        bias_copy(step).wait()
        bias_total = bias_total + bias_from[step]
    bias_keep[...] = bias_total
    keep = pltpu.make_async_copy(bias_keep, bias_sum, store.at[2])
    keep.start()
    keep.wait()
    hand.wait()
    pltpu.make_async_copy(held_in, tiles_in, store.at[0]).wait()
    pltpu.make_async_copy(held_out, tiles_out, store.at[1]).wait()


def local(
    activations, out_grads, w_in, w_out, bias_in, cols_in, mask_in, cols_out, mask_out, block_rows
):
    tensor = lax.axis_size("tensor")
    sections = lax.axis_size("section")
    chips = tensor // 2
    _, rows, slots = cols_in.shape
    depth = activations.shape[1]
    per = depth // BLK
    dblocks = per * tensor
    hblocks = rows * tensor
    any_spec = pl.BlockSpec(memory_space=pl.ANY)
    vmem_spec = pl.BlockSpec(memory_space=pltpu.VMEM)
    smem_spec = pl.BlockSpec(memory_space=pltpu.SMEM)
    dma = pltpu.SemaphoreType.DMA

    act_all, grad_all, bias_all = pl.pallas_call(
        functools.partial(gather_kernel, tensor),
        out_shape=(
            jax.ShapeDtypeStruct((tensor, per, BLK, BLK), BF16),
            jax.ShapeDtypeStruct((tensor, per, BLK, BLK), BF16),
            jax.ShapeDtypeStruct((tensor, rows, BLK), BF16),
        ),
        in_specs=[any_spec] * 3,
        out_specs=[any_spec] * 3,
        scratch_shapes=[dma((3, chips))] * 4 + [dma((3,))],
        compiler_params=pltpu.CompilerParams(collective_id=0, has_side_effects=True),
        name="gather_inputs",
    )(
        activations.reshape(per, BLK, BLK),
        out_grads.reshape(per, BLK, BLK),
        bias_in.reshape(rows, BLK),
    )
    act_all = act_all.reshape(dblocks, BLK, BLK)
    grad_all = grad_all.reshape(dblocks, BLK, BLK)

    def whole(*shape):
        return pl.BlockSpec(shape, lambda row, *_: (0,) * len(shape))

    tile_spec = pl.BlockSpec((1, slots, BLK, BLK), lambda row, *_: (row, 0, 0, 0))
    block_spec = pl.BlockSpec((1, BLK, BLK), lambda row, *_: (row, 0, 0))
    hidden, low, part, bias_part = pl.pallas_call(
        functools.partial(row_kernel, slots, rows, dblocks, tensor),
        out_shape=(
            jax.ShapeDtypeStruct((rows, BLK, BLK), BF16),
            jax.ShapeDtypeStruct((rows, BLK, BLK), BF16),
            jax.ShapeDtypeStruct((2, chips, per, BLK, BLK), BF16),
            jax.ShapeDtypeStruct((hblocks, BLK), F32),
        ),
        grid_spec=pltpu.PrefetchScalarGridSpec(
            num_scalar_prefetch=5,
            grid=(rows,),
            in_specs=[
                tile_spec,
                tile_spec,
                whole(dblocks, BLK, BLK),
                whole(dblocks, BLK, BLK),
                whole(tensor, rows, BLK),
            ],
            out_specs=[
                block_spec,
                block_spec,
                whole(2, chips, per, BLK, BLK),
                whole(hblocks, BLK),
            ],
            scratch_shapes=[
                pltpu.VMEM((dblocks, BLK, BLK), F32),
                pltpu.VMEM((hblocks, BLK), F32),
            ],
        ),
        compiler_params=pltpu.CompilerParams(vmem_limit_bytes=48 << 20),
        name="rows",
    )(
        cols_in[0], mask_in[0], cols_out[0], mask_out[0], block_rows[0],
        w_in[0], w_out[0], act_all, grad_all, bias_all,
    )

    tiles_in, tiles_out, bias_sum, handed = pl.pallas_call(
        functools.partial(scatter_kernel, tensor, sections, slots, rows, per),
        out_shape=(
            jax.ShapeDtypeStruct((rows, slots, BLK, BLK), BF16),
            jax.ShapeDtypeStruct((rows, slots, BLK, BLK), BF16),
            jax.ShapeDtypeStruct((rows, BLK), F32),
            jax.ShapeDtypeStruct((per, BLK, BLK), BF16),
        ),
        in_specs=[smem_spec] * 4 + [vmem_spec] * 6,
        out_specs=[any_spec] * 4,
        scratch_shapes=[
            pltpu.VMEM((rows, slots, BLK, BLK), BF16),
            pltpu.VMEM((rows, slots, BLK, BLK), BF16),
            pltpu.VMEM((chips, per, BLK, BLK), BF16),
            pltpu.VMEM((chips, per, BLK, BLK), BF16),
            pltpu.VMEM((chips, per, BLK, BLK), BF16),
            pltpu.VMEM((per, BLK, BLK), BF16),
            pltpu.VMEM((tensor, rows, BLK), F32),
            pltpu.VMEM((rows, BLK), F32),
            dma(()), dma(()),
            dma((chips,)), dma((chips,)),
            dma((tensor,)), dma((tensor,)),
            dma(()), dma(()),
            dma((3,)),
        ],
        compiler_params=pltpu.CompilerParams(
            collective_id=1, has_side_effects=True, vmem_limit_bytes=48 << 20
        ),
        name="scatter_tiles",
    )(
        cols_in[0], mask_in[0], cols_out[0], mask_out[0],
        part, bias_part.reshape(tensor, rows, BLK), hidden, low, act_all, grad_all,
    )
    return (
        tiles_in[None],
        tiles_out[None],
        bias_sum.reshape(1, rows * BLK),
        handed.reshape(1, depth, BLK),
    )


def solution(mesh):
    return jax.shard_map(
        local,
        mesh=mesh,
        in_specs=(
            P("section", "tensor", None),
            P("section", "tensor", None),
            P("section", "tensor", None, None, None),
            P("section", "tensor", None, None, None),
            P("section", "tensor"),
            P("section", "tensor", None),
            P("section", "tensor", None),
            P("section", "tensor", None),
            P("section", "tensor", None),
            P("section", "tensor"),
        ),
        out_specs=(
            P("section", "tensor", None, None, None),
            P("section", "tensor", None, None, None),
            P("section", "tensor"),
            P("section", "tensor", None),
        ),
        check_vma=False,
    )
```

```python
import functools

import jax
import jax.numpy as jnp
from jax import lax
from jax.experimental import pallas as pl
from jax.experimental.pallas import tpu as pltpu
from jax.sharding import PartitionSpec as P

BLK = 128
MESH = pl.DeviceIdType.MESH
BF16 = jnp.bfloat16
F32 = jnp.float32


def gelu_parts(pre_act):
    cdf_part = 0.5 * (1.0 + lax.erf(pre_act * 0.7071067811865476))
    density = jnp.exp(-0.5 * pre_act * pre_act) * 0.3989422804014327
    return (pre_act * cdf_part, cdf_part + pre_act * density)


def gather_kernel(
    tensor, act, grad, bias, act_all, grad_all, bias_all, send, recv, fsend, frecv, own
):
    chips = tensor // 2
    me = lax.axis_index("tensor")
    sec = lax.axis_index("section")
    core = lax.rem(me, 2)
    chip = me // 2
    partner = chip * 2 + (1 - core)
    sources = (act, grad, bias)
    results = (act_all, grad_all, bias_all)

    def other(step):
        return lax.rem(chip + step, chips) * 2 + core

    def behind(step):
        return lax.rem(chip + chips - step, chips) * 2 + core

    barrier = pltpu.get_barrier_semaphore()
    for peer in [partner] + [other(step) for step in range(1, chips)]:
        pl.semaphore_signal(barrier, inc=1, device_id=(sec, peer), device_id_type=MESH)
    pl.semaphore_wait(barrier, chips)

    def far(kind, step):
        return pltpu.make_async_remote_copy(
            src_ref=sources[kind],
            dst_ref=results[kind].at[me],
            send_sem=send.at[kind, step],
            recv_sem=recv.at[kind, step],
            device_id=(sec, other(step)),
            device_id_type=MESH,
        )

    def near(kind, step):
        slot = behind(step)
        return pltpu.make_async_remote_copy(
            src_ref=sources[kind] if step == 0 else results[kind].at[slot],
            dst_ref=results[kind].at[slot],
            send_sem=fsend.at[kind, step],
            recv_sem=frecv.at[kind, step],
            device_id=(sec, partner),
            device_id_type=MESH,
        )

    order = (2, 0, 1)
    for kind in order:
        for step in range(1, chips):
            far(kind, step).start()
    for kind in order:
        near(kind, 0).start()
        pltpu.make_async_copy(sources[kind], results[kind].at[me], own.at[kind]).start()
    for kind in order:
        for step in range(1, chips):
            far(kind, step).wait_recv()
            near(kind, step).start()
    for kind in order:
        pltpu.make_async_copy(sources[kind], results[kind].at[me], own.at[kind]).wait()
        for step in range(1, chips):
            far(kind, step).wait_send()
        for step in range(chips):
            near(kind, step).wait()


def tall(ref, meta, row, slots, first):
    return jnp.concatenate(
        [
            jnp.where(
                meta[first + slots + s, row] > 0,
                ref[meta[first + s, row]],
                jnp.zeros((BLK, BLK), BF16),
            )
            for s in range(slots)
        ],
        axis=0,
    )


def row_kernel(
    slots, group, dblocks, tensor,
    meta, stored,
    w_in, w_out, act, grad, bias,
    hidden_out, low_out, part_out, bias_out,
    total, bias_wide,
):
    step = pl.program_id(0)
    hblocks = bias_wide.shape[0]

    @pl.when(step == 0)
    def _():
        total[...] = jnp.zeros_like(total)
        bias_out[...] = jnp.zeros_like(bias_out)
        bias_wide[...] = bias[...].reshape(hblocks, BLK).astype(F32)

    def wide(ref, g):
        return jnp.concatenate([ref[g, s] for s in range(slots)], axis=1)

    several = range(group)
    line = [step * group + g for g in several]
    where_row = [stored[line[g]] for g in several]
    pre_act = []
    for g in several:
        bias_row = bias_wide[pl.ds(where_row[g], 1), :]
        bias_col = jnp.transpose(jnp.broadcast_to(bias_row, (BLK, BLK)))
        pre_act.append(
            jnp.dot(
                wide(w_in, g), tall(act, meta, line[g], slots, 0), preferred_element_type=F32
            )
            + bias_col
        )
    grad_hidden = [
        jnp.dot(
            wide(w_out, g), tall(grad, meta, line[g], slots, 2 * slots), preferred_element_type=F32
        )
        for g in several
    ]
    turned = []
    for g in several:
        act_value, slope = gelu_parts(pre_act[g])
        hidden_out[g] = act_value.astype(BF16)
        grad_pre = grad_hidden[g] * slope
        low_out[g] = grad_pre.astype(BF16)
        turned.append(jnp.transpose(grad_pre))
    pieces = [
        jnp.dot(turned[g].astype(BF16), wide(w_in, g), preferred_element_type=F32) for g in several
    ]
    for g in several:
        bias_out[pl.ds(where_row[g], 1), :] = jnp.sum(turned[g], axis=0, keepdims=True)
        for s in range(slots):
            piece = pieces[g][:, s * BLK : (s + 1) * BLK]
            total[meta[s, line[g]]] += jnp.where(meta[slots + s, line[g]] > 0, piece, 0.0)

    @pl.when(step == pl.num_programs(0) - 1)
    def _():
        chips = tensor // 2
        per = dblocks // tensor
        for chip in range(chips):
            for core in range(2):
                base = (chip * 2 + core) * per
                part_out[core, chip] = total[base : base + per].astype(BF16)


def scatter_kernel(
    tensor, sections, slots, rows, per,
    meta,
    part, bias_part, hidden, low, act, grad,
    tiles_in, tiles_out, bias_sum, handed,
    from_pair, pair_sum, from_chips, final, bias_from,
    pair_send, pair_recv, chip_send, chip_recv, bias_send, bias_recv, hand_send, hand_recv,
):
    chips = tensor // 2
    me = lax.axis_index("tensor")
    sec = lax.axis_index("section")
    core = lax.rem(me, 2)
    chip = me // 2
    partner = chip * 2 + (1 - core)
    before = lax.rem(sec + sections - 1, sections)
    after = lax.rem(sec + 1, sections)

    def ahead_chip(step):
        return lax.rem(chip + step, chips)

    barrier = pltpu.get_barrier_semaphore()
    for step in range(1, tensor):
        pl.semaphore_signal(
            barrier, inc=1, device_id=(sec, lax.rem(me + step, tensor)), device_id_type=MESH
        )
    for section in (before, after):
        pl.semaphore_signal(barrier, inc=1, device_id=(section, me), device_id_type=MESH)
    pl.semaphore_wait(barrier, tensor + 1)

    pair = pltpu.make_async_remote_copy(
        src_ref=part.at[1 - core],
        dst_ref=from_pair,
        send_sem=pair_send,
        recv_sem=pair_recv,
        device_id=(sec, partner),
        device_id_type=MESH,
    )
    pair.start()

    def bias_copy(step):
        peer = lax.rem(me + step, tensor)
        return pltpu.make_async_remote_copy(
            src_ref=bias_part.at[peer],
            dst_ref=bias_from.at[step],
            send_sem=bias_send.at[step],
            recv_sem=bias_recv.at[step],
            device_id=(sec, peer),
            device_id_type=MESH,
        )

    for step in range(1, tensor):
        bias_copy(step).start()

    def chip_copy(step):
        return pltpu.make_async_remote_copy(
            src_ref=pair_sum.at[step],
            dst_ref=from_chips.at[step],
            send_sem=chip_send.at[step],
            recv_sem=chip_recv.at[step],
            device_id=(sec, ahead_chip(step) * 2 + core),
            device_id_type=MESH,
        )

    def out_product(left, right):
        return lax.dot_general(
            left, right, (((1,), (1,)), ((), ())), preferred_element_type=F32
        ).astype(BF16)

    def one_row(row, carry):
        got_in = out_product(low[row], tall(act, meta, row, slots, 0))
        got_out = out_product(hidden[row], tall(grad, meta, row, slots, 2 * slots))
        for s in range(slots):
            tiles_in[row, s] = got_in[:, s * BLK : (s + 1) * BLK]
            tiles_out[row, s] = got_out[:, s * BLK : (s + 1) * BLK]
        return carry

    first, second = rows // 4, rows - rows // 4
    lax.fori_loop(0, first, one_row, 0)

    pair.wait()
    for step in list(range(1, chips)) + [0]:
        where_chip = ahead_chip(step)
        pair_sum[step] = (
            part[core, where_chip].astype(F32) + from_pair[where_chip].astype(F32)
        ).astype(BF16)
        if step:
            chip_copy(step).start()

    lax.fori_loop(first, second, one_row, 0)

    result = pair_sum[0].astype(F32)
    for step in range(1, chips):
        chip_copy(step).wait()
        result = result + from_chips[step].astype(F32)
    for block in range(per):
        final[block] = jnp.transpose(result[block]).astype(BF16)
    hand = pltpu.make_async_remote_copy(
        src_ref=final,
        dst_ref=handed,
        send_sem=hand_send,
        recv_sem=hand_recv,
        device_id=(before, me),
        device_id_type=MESH,
    )
    hand.start()

    lax.fori_loop(second, rows, one_row, 0)

    bias_total = bias_part[me]
    for step in range(1, tensor):
        bias_copy(step).wait()
        bias_total = bias_total + bias_from[step]
    bias_sum[...] = bias_total
    hand.wait()


def local(
    activations, out_grads, w_in, w_out, bias_in, cols_in, mask_in, cols_out, mask_out, block_rows
):
    tensor = lax.axis_size("tensor")
    sections = lax.axis_size("section")
    chips = tensor // 2
    _, rows, slots = cols_in.shape
    depth = activations.shape[1]
    per = depth // BLK
    dblocks = per * tensor
    hblocks = rows * tensor
    group = 4 if rows % 4 == 0 else 1
    meta = jnp.concatenate([cols_in[0].T, mask_in[0].T, cols_out[0].T, mask_out[0].T], axis=0)
    any_spec = pl.BlockSpec(memory_space=pl.ANY)
    vmem_spec = pl.BlockSpec(memory_space=pltpu.VMEM)
    smem_spec = pl.BlockSpec(memory_space=pltpu.SMEM)
    dma = pltpu.SemaphoreType.DMA

    act_all, grad_all, bias_all = pl.pallas_call(
        functools.partial(gather_kernel, tensor),
        out_shape=(
            jax.ShapeDtypeStruct((tensor, per, BLK, BLK), BF16),
            jax.ShapeDtypeStruct((tensor, per, BLK, BLK), BF16),
            jax.ShapeDtypeStruct((tensor, rows, BLK), BF16),
        ),
        in_specs=[any_spec] * 3,
        out_specs=[vmem_spec] * 3,
        scratch_shapes=[dma((3, chips))] * 4 + [dma((3,))],
        compiler_params=pltpu.CompilerParams(
            collective_id=0, has_side_effects=True, vmem_limit_bytes=16 << 20
        ),
        name="gather_inputs",
    )(
        activations.reshape(per, BLK, BLK),
        out_grads.reshape(per, BLK, BLK),
        bias_in.reshape(rows, BLK),
    )
    act_all = act_all.reshape(dblocks, BLK, BLK)
    grad_all = grad_all.reshape(dblocks, BLK, BLK)

    def whole(*shape):
        return pl.BlockSpec(shape, lambda row, *_: (0,) * len(shape))

    tile_spec = pl.BlockSpec((group, slots, BLK, BLK), lambda row, *_: (row, 0, 0, 0))
    block_spec = pl.BlockSpec((group, BLK, BLK), lambda row, *_: (row, 0, 0))
    hidden, low, part, bias_part = pl.pallas_call(
        functools.partial(row_kernel, slots, group, dblocks, tensor),
        out_shape=(
            jax.ShapeDtypeStruct((rows, BLK, BLK), BF16),
            jax.ShapeDtypeStruct((rows, BLK, BLK), BF16),
            jax.ShapeDtypeStruct((2, chips, per, BLK, BLK), BF16),
            jax.ShapeDtypeStruct((hblocks, BLK), F32),
        ),
        grid_spec=pltpu.PrefetchScalarGridSpec(
            num_scalar_prefetch=2,
            grid=(rows // group,),
            in_specs=[
                tile_spec,
                tile_spec,
                whole(dblocks, BLK, BLK),
                whole(dblocks, BLK, BLK),
                whole(tensor, rows, BLK),
            ],
            out_specs=[
                block_spec,
                block_spec,
                whole(2, chips, per, BLK, BLK),
                whole(hblocks, BLK),
            ],
            scratch_shapes=[
                pltpu.VMEM((dblocks, BLK, BLK), F32),
                pltpu.VMEM((hblocks, BLK), F32),
            ],
        ),
        compiler_params=pltpu.CompilerParams(vmem_limit_bytes=42 << 20),
        name="rows",
    )(
        meta, block_rows[0],
        w_in[0], w_out[0], act_all, grad_all, bias_all,
    )

    tiles_in, tiles_out, bias_sum, handed = pl.pallas_call(
        functools.partial(scatter_kernel, tensor, sections, slots, rows, per),
        out_shape=(
            jax.ShapeDtypeStruct((rows, slots, BLK, BLK), BF16),
            jax.ShapeDtypeStruct((rows, slots, BLK, BLK), BF16),
            jax.ShapeDtypeStruct((rows, BLK), F32),
            jax.ShapeDtypeStruct((per, BLK, BLK), BF16),
        ),
        in_specs=[smem_spec] + [vmem_spec] * 6,
        out_specs=[vmem_spec] * 4,
        scratch_shapes=[
            pltpu.VMEM((chips, per, BLK, BLK), BF16),
            pltpu.VMEM((chips, per, BLK, BLK), BF16),
            pltpu.VMEM((chips, per, BLK, BLK), BF16),
            pltpu.VMEM((per, BLK, BLK), BF16),
            pltpu.VMEM((tensor, rows, BLK), F32),
            dma(()), dma(()),
            dma((chips,)), dma((chips,)),
            dma((tensor,)), dma((tensor,)),
            dma(()), dma(()),
        ],
        compiler_params=pltpu.CompilerParams(
            collective_id=1, has_side_effects=True, vmem_limit_bytes=16 << 20
        ),
        name="scatter_tiles",
    )(
        meta,
        part, bias_part.reshape(tensor, rows, BLK), hidden, low, act_all, grad_all,
    )
    return (
        tiles_in[None],
        tiles_out[None],
        bias_sum.reshape(1, rows * BLK),
        handed.reshape(1, depth, BLK),
    )


def solution(mesh):
    return jax.shard_map(
        local,
        mesh=mesh,
        in_specs=(
            P("section", "tensor", None),
            P("section", "tensor", None),
            P("section", "tensor", None, None, None),
            P("section", "tensor", None, None, None),
            P("section", "tensor"),
            P("section", "tensor", None),
            P("section", "tensor", None),
            P("section", "tensor", None),
            P("section", "tensor", None),
            P("section", "tensor"),
        ),
        out_specs=(
            P("section", "tensor", None, None, None),
            P("section", "tensor", None, None, None),
            P("section", "tensor"),
            P("section", "tensor", None),
        ),
        check_vma=False,
    )
```

```python
import functools

import jax
import jax.numpy as jnp
from jax import lax
from jax.experimental import pallas as pl
from jax.experimental.pallas import tpu as pltpu
from jax.sharding import PartitionSpec as P

BLK = 128
MESH = pl.DeviceIdType.MESH
BF16 = jnp.bfloat16
F32 = jnp.float32


def gelu_parts(pre_act):
    cdf_part = 0.5 * (1.0 + lax.erf(pre_act * 0.7071067811865476))
    density = jnp.exp(-0.5 * pre_act * pre_act) * 0.3989422804014327
    return (pre_act * cdf_part, cdf_part + pre_act * density)


def gather_kernel(
    tensor, act, grad, bias, act_all, grad_all, bias_all, send, recv, fsend, frecv, own
):
    chips = tensor // 2
    me = lax.axis_index("tensor")
    sec = lax.axis_index("section")
    core = lax.rem(me, 2)
    chip = me // 2
    partner = chip * 2 + (1 - core)
    sources = (act, grad, bias)
    results = (act_all, grad_all, bias_all)

    def other(step):
        return lax.rem(chip + step, chips) * 2 + core

    def behind(step):
        return lax.rem(chip + chips - step, chips) * 2 + core

    barrier = pltpu.get_barrier_semaphore()
    for peer in [partner] + [other(step) for step in range(1, chips)]:
        pl.semaphore_signal(barrier, inc=1, device_id=(sec, peer), device_id_type=MESH)
    pl.semaphore_wait(barrier, chips)

    def far(kind, step):
        return pltpu.make_async_remote_copy(
            src_ref=sources[kind],
            dst_ref=results[kind].at[me],
            send_sem=send.at[kind, step],
            recv_sem=recv.at[kind, step],
            device_id=(sec, other(step)),
            device_id_type=MESH,
        )

    def near(kind, step):
        slot = behind(step)
        return pltpu.make_async_remote_copy(
            src_ref=sources[kind] if step == 0 else results[kind].at[slot],
            dst_ref=results[kind].at[slot],
            send_sem=fsend.at[kind, step],
            recv_sem=frecv.at[kind, step],
            device_id=(sec, partner),
            device_id_type=MESH,
        )

    everything = [(kind, step) for kind in (2, 0, 1) for step in range(1, chips)]
    if chips == 4:
        low_bit = lax.rem(chip, 2)
        side = chip + 1 - 2 * low_bit
        over = lax.rem(chip + 2, chips)
        across = lax.rem(side + 2, chips)

        def link(kind, step):
            return pltpu.make_async_remote_copy(
                src_ref=results[kind].at[(side, over)[kind] * 2 + core] if step == 3 else sources[kind],
                dst_ref=results[kind].at[((side, over)[kind] * 2 + core) if step == 3 else me],
                send_sem=send.at[kind, step],
                recv_sem=recv.at[kind, step],
                device_id=(sec, ((over, side)[kind] if step == 3 else (side, over)[step - 1]) * 2 + core),
                device_id_type=MESH,
            )

        def pass_on(kind, step):
            slot = (side, over, across)[step - 1] * 2 + core
            return pltpu.make_async_remote_copy(
                src_ref=results[kind].at[slot],
                dst_ref=results[kind].at[slot],
                send_sem=fsend.at[kind, step],
                recv_sem=frecv.at[kind, step],
                device_id=(sec, partner),
                device_id_type=MESH,
            )

        first = [(0, 1), (1, 2), (1, 1), (0, 2)]
        for kind, step in first:
            link(kind, step).start()
        for step in range(1, chips):
            far(2, step).start()
        for kind in (0, 1, 2):
            near(kind, 0).start()
            pltpu.make_async_copy(sources[kind], results[kind].at[me], own.at[kind]).start()
        for kind, step in first:
            link(kind, step).wait_recv()
            if step == kind + 1:
                link(kind, 3).start()
            pass_on(kind, step).start()
        for step in range(1, chips):
            far(2, step).wait_recv()
            near(2, step).start()
        for kind in (0, 1):
            link(kind, 3).wait_recv()
            pass_on(kind, 3).start()
        for kind in (0, 1):
            for step in range(1, chips):
                link(kind, step).wait_send()
                pass_on(kind, step).wait()
        for step in range(1, chips):
            far(2, step).wait_send()
            near(2, step).wait()
    else:
        for kind, step in everything:
            far(kind, step).start()
        for kind in (2, 0, 1):
            near(kind, 0).start()
            pltpu.make_async_copy(sources[kind], results[kind].at[me], own.at[kind]).start()
        for kind, step in everything:
            far(kind, step).wait_recv()
            near(kind, step).start()
        for kind, step in everything:
            far(kind, step).wait_send()
            near(kind, step).wait()
    for kind in (0, 1, 2):
        pltpu.make_async_copy(sources[kind], results[kind].at[me], own.at[kind]).wait()
        near(kind, 0).wait()


def tall(ref, meta, row, slots, first):
    return jnp.concatenate(
        [
            jnp.where(
                meta[first + slots + s, row] > 0,
                ref[meta[first + s, row]],
                jnp.zeros((BLK, BLK), BF16),
            )
            for s in range(slots)
        ],
        axis=0,
    )


def row_kernel(
    slots, group, dblocks, tensor,
    meta,
    w_in, w_out, act, grad, bias,
    hidden_out, low_out, part_out, bias_out,
    total, bias_wide,
):
    step = pl.program_id(0)
    hblocks = bias_wide.shape[0]

    @pl.when(step == 0)
    def _():
        total[...] = jnp.zeros_like(total)
        bias_out[...] = jnp.zeros_like(bias_out)
        bias_wide[...] = bias[...].reshape(hblocks, BLK).astype(F32)

    def wide(ref, g):
        return jnp.concatenate([ref[g, s] for s in range(slots)], axis=1)

    several = range(group)
    line = [step * group + g for g in several]
    where_row = [meta[4 * slots, line[g]] for g in several]
    pre_act = []
    for g in several:
        bias_row = bias_wide[pl.ds(where_row[g], 1), :]
        bias_col = jnp.transpose(jnp.broadcast_to(bias_row, (BLK, BLK)))
        pre_act.append(
            jnp.dot(
                wide(w_in, g), tall(act, meta, line[g], slots, 0), preferred_element_type=F32
            )
            + bias_col
        )
    grad_hidden = [
        jnp.dot(
            wide(w_out, g), tall(grad, meta, line[g], slots, 2 * slots), preferred_element_type=F32
        )
        for g in several
    ]
    turned = []
    for g in several:
        act_value, slope = gelu_parts(pre_act[g])
        hidden_out[g] = act_value.astype(BF16)
        grad_pre = grad_hidden[g] * slope
        low_out[g] = grad_pre.astype(BF16)
        turned.append(jnp.transpose(grad_pre))
    pieces = [
        jnp.dot(turned[g].astype(BF16), wide(w_in, g), preferred_element_type=F32) for g in several
    ]
    for g in several:
        bias_out[pl.ds(where_row[g], 1), :] = jnp.sum(turned[g], axis=0, keepdims=True)
        for s in range(slots):
            piece = pieces[g][:, s * BLK : (s + 1) * BLK]
            total[meta[s, line[g]]] += jnp.where(meta[slots + s, line[g]] > 0, piece, 0.0)

    @pl.when(step == pl.num_programs(0) - 1)
    def _():
        chips = tensor // 2
        per = dblocks // tensor
        for chip in range(chips):
            for core in range(2):
                base = (chip * 2 + core) * per
                part_out[core, chip] = total[base : base + per].astype(BF16)


def scatter_kernel(
    tensor, sections, slots, rows, per, parts,
    meta,
    part, bias_part, hidden, low, act, grad,
    tiles_in, tiles_out, bias_sum, handed,
    from_pair, pair_sum, from_chips, final, bias_from,
    pair_send, pair_recv, chip_send, chip_recv, bias_send, bias_recv, hand_send, hand_recv,
):
    chips = tensor // 2
    me = lax.axis_index("tensor")
    sec = lax.axis_index("section")
    core = lax.rem(me, 2)
    chip = me // 2
    partner = chip * 2 + (1 - core)
    before = lax.rem(sec + sections - 1, sections)
    after = lax.rem(sec + 1, sections)

    def ahead_chip(step):
        return lax.rem(chip + step, chips)

    barrier = pltpu.get_barrier_semaphore()
    for step in range(1, tensor):
        pl.semaphore_signal(
            barrier, inc=1, device_id=(sec, lax.rem(me + step, tensor)), device_id_type=MESH
        )
    for section in (before, after):
        pl.semaphore_signal(barrier, inc=1, device_id=(section, me), device_id_type=MESH)
    pl.semaphore_wait(barrier, tensor + 1)

    size = per // parts

    def pair(part_no):
        blocks = pl.ds(part_no * size, size)
        return pltpu.make_async_remote_copy(
            src_ref=part.at[1 - core, :, blocks],
            dst_ref=from_pair.at[:, blocks],
            send_sem=pair_send.at[part_no],
            recv_sem=pair_recv.at[part_no],
            device_id=(sec, partner),
            device_id_type=MESH,
        )

    for part_no in range(parts):
        pair(part_no).start()

    def bias_copy(step):
        peer = lax.rem(me + step, tensor)
        return pltpu.make_async_remote_copy(
            src_ref=bias_part.at[peer],
            dst_ref=bias_from.at[step],
            send_sem=bias_send.at[step],
            recv_sem=bias_recv.at[step],
            device_id=(sec, peer),
            device_id_type=MESH,
        )

    for step in range(1, tensor):
        bias_copy(step).start()

    def chip_copy(part_no, step):
        blocks = pl.ds(part_no * size, size)
        return pltpu.make_async_remote_copy(
            src_ref=pair_sum.at[step, blocks],
            dst_ref=from_chips.at[step, blocks],
            send_sem=chip_send.at[part_no, step],
            recv_sem=chip_recv.at[part_no, step],
            device_id=(sec, ahead_chip(step) * 2 + core),
            device_id_type=MESH,
        )

    def hand(part_no):
        blocks = pl.ds(part_no * size, size)
        return pltpu.make_async_remote_copy(
            src_ref=final.at[blocks],
            dst_ref=handed.at[blocks],
            send_sem=hand_send.at[part_no],
            recv_sem=hand_recv.at[part_no],
            device_id=(before, me),
            device_id_type=MESH,
        )

    def out_product(left, right):
        return lax.dot_general(
            left, right, (((1,), (1,)), ((), ())), preferred_element_type=F32
        ).astype(BF16)

    def one_row(row, carry):
        got_in = out_product(low[row], tall(act, meta, row, slots, 0))
        got_out = out_product(hidden[row], tall(grad, meta, row, slots, 2 * slots))
        for s in range(slots):
            tiles_in[row, s] = got_in[:, s * BLK : (s + 1) * BLK]
            tiles_out[row, s] = got_out[:, s * BLK : (s + 1) * BLK]
        return carry

    marks = [0]

    def compute_to(share):
        goal = (rows * share) // 32
        lax.fori_loop(marks[-1], goal, one_row, 0)
        marks.append(goal)

    for part_no in range(parts):
        compute_to((part_no + 1) * 4 // parts)
        pair(part_no).wait()
        mine = slice(part_no * size, (part_no + 1) * size)
        for step in list(range(1, chips)) + [0]:
            where_chip = ahead_chip(step)
            pair_sum[step, mine] = (
                part[core, where_chip, mine].astype(F32) + from_pair[where_chip, mine].astype(F32)
            ).astype(BF16)
            if step:
                chip_copy(part_no, step).start()

    for part_no in range(parts):
        compute_to(4 + (part_no + 1) * 24 // parts)
        mine = slice(part_no * size, (part_no + 1) * size)
        result = pair_sum[0, mine].astype(F32)
        for step in range(1, chips):
            chip_copy(part_no, step).wait()
            result = result + from_chips[step, mine].astype(F32)
        for block in range(size):
            final[part_no * size + block] = jnp.transpose(result[block]).astype(BF16)
        hand(part_no).start()

    compute_to(32)

    bias_total = bias_part[me]
    for step in range(1, tensor):
        bias_copy(step).wait()
        bias_total = bias_total + bias_from[step]
    bias_sum[...] = bias_total
    for part_no in range(parts):
        hand(part_no).wait()


def local(
    activations, out_grads, w_in, w_out, bias_in, cols_in, mask_in, cols_out, mask_out, block_rows
):
    tensor = lax.axis_size("tensor")
    sections = lax.axis_size("section")
    chips = tensor // 2
    _, rows, slots = cols_in.shape
    depth = activations.shape[1]
    per = depth // BLK
    dblocks = per * tensor
    hblocks = rows * tensor
    group = 4 if rows % 4 == 0 else 1
    parts = 4 if per % 4 == 0 else 1
    meta = jnp.concatenate(
        [cols_in[0].T, mask_in[0].T, cols_out[0].T, mask_out[0].T, block_rows], axis=0
    )
    vmem_spec = pl.BlockSpec(memory_space=pltpu.VMEM)
    smem_spec = pl.BlockSpec(memory_space=pltpu.SMEM)
    dma = pltpu.SemaphoreType.DMA

    act_all, grad_all, bias_all = pl.pallas_call(
        functools.partial(gather_kernel, tensor),
        out_shape=(
            jax.ShapeDtypeStruct((tensor, per, BLK, BLK), BF16),
            jax.ShapeDtypeStruct((tensor, per, BLK, BLK), BF16),
            jax.ShapeDtypeStruct((tensor, rows, BLK), BF16),
        ),
        in_specs=[pl.BlockSpec(memory_space=pltpu.HBM)] * 3,
        out_specs=[vmem_spec] * 3,
        scratch_shapes=[dma((3, chips))] * 4 + [dma((3,))],
        compiler_params=pltpu.CompilerParams(
            collective_id=0, has_side_effects=True, vmem_limit_bytes=16 << 20
        ),
        name="gather_inputs",
    )(
        activations.reshape(per, BLK, BLK),
        out_grads.reshape(per, BLK, BLK),
        bias_in.reshape(rows, BLK),
    )
    act_all = act_all.reshape(dblocks, BLK, BLK)
    grad_all = grad_all.reshape(dblocks, BLK, BLK)

    def whole(*shape):
        return pl.BlockSpec(shape, lambda row, *_: (0,) * len(shape))

    tile_spec = pl.BlockSpec((group, slots, BLK, BLK), lambda row, *_: (row, 0, 0, 0))
    block_spec = pl.BlockSpec((group, BLK, BLK), lambda row, *_: (row, 0, 0))
    hidden, low, part, bias_part = pl.pallas_call(
        functools.partial(row_kernel, slots, group, dblocks, tensor),
        out_shape=(
            jax.ShapeDtypeStruct((rows, BLK, BLK), BF16),
            jax.ShapeDtypeStruct((rows, BLK, BLK), BF16),
            jax.ShapeDtypeStruct((2, chips, per, BLK, BLK), BF16),
            jax.ShapeDtypeStruct((hblocks, BLK), F32),
        ),
        grid_spec=pltpu.PrefetchScalarGridSpec(
            num_scalar_prefetch=1,
            grid=(rows // group,),
            in_specs=[
                tile_spec,
                tile_spec,
                whole(dblocks, BLK, BLK),
                whole(dblocks, BLK, BLK),
                whole(tensor, rows, BLK),
            ],
            out_specs=[
                block_spec,
                block_spec,
                whole(2, chips, per, BLK, BLK),
                whole(hblocks, BLK),
            ],
            scratch_shapes=[
                pltpu.VMEM((dblocks, BLK, BLK), F32),
                pltpu.VMEM((hblocks, BLK), F32),
            ],
        ),
        compiler_params=pltpu.CompilerParams(vmem_limit_bytes=42 << 20),
        name="rows",
    )(
        meta,
        w_in[0], w_out[0], act_all, grad_all, bias_all,
    )

    tiles_in, tiles_out, bias_sum, handed = pl.pallas_call(
        functools.partial(scatter_kernel, tensor, sections, slots, rows, per, parts),
        out_shape=(
            jax.ShapeDtypeStruct((rows, slots, BLK, BLK), BF16),
            jax.ShapeDtypeStruct((rows, slots, BLK, BLK), BF16),
            jax.ShapeDtypeStruct((rows, BLK), F32),
            jax.ShapeDtypeStruct((per, BLK, BLK), BF16),
        ),
        in_specs=[smem_spec] + [vmem_spec] * 6,
        out_specs=[vmem_spec] * 4,
        scratch_shapes=[
            pltpu.VMEM((chips, per, BLK, BLK), BF16),
            pltpu.VMEM((chips, per, BLK, BLK), BF16),
            pltpu.VMEM((chips, per, BLK, BLK), BF16),
            pltpu.VMEM((per, BLK, BLK), BF16),
            pltpu.VMEM((tensor, rows, BLK), F32),
            dma((parts,)), dma((parts,)),
            dma((parts, chips)), dma((parts, chips)),
            dma((tensor,)), dma((tensor,)),
            dma((parts,)), dma((parts,)),
        ],
        compiler_params=pltpu.CompilerParams(
            collective_id=1, has_side_effects=True, vmem_limit_bytes=16 << 20
        ),
        name="scatter_tiles",
    )(
        meta,
        part, bias_part.reshape(tensor, rows, BLK), hidden, low, act_all, grad_all,
    )
    return (
        tiles_in[None],
        tiles_out[None],
        bias_sum.reshape(1, rows * BLK),
        handed.reshape(1, depth, BLK),
    )


def solution(mesh):
    return jax.shard_map(
        local,
        mesh=mesh,
        in_specs=(
            P("section", "tensor", None),
            P("section", "tensor", None),
            P("section", "tensor", None, None, None),
            P("section", "tensor", None, None, None),
            P("section", "tensor"),
            P("section", "tensor", None),
            P("section", "tensor", None),
            P("section", "tensor", None),
            P("section", "tensor", None),
            P("section", "tensor"),
        ),
        out_specs=(
            P("section", "tensor", None, None, None),
            P("section", "tensor", None, None, None),
            P("section", "tensor"),
            P("section", "tensor", None),
        ),
        check_vma=False,
    )
```

```python
import functools

import jax
import jax.numpy as jnp
from jax import lax
from jax.experimental import pallas as pl
from jax.experimental.pallas import tpu as pltpu
from jax.sharding import PartitionSpec as P

BLK = 128
MESH = pl.DeviceIdType.MESH
BF16 = jnp.bfloat16
F32 = jnp.float32


def gelu_parts(pre_act):
    cdf_part = 0.5 * (1.0 + lax.erf(pre_act * 0.7071067811865476))
    density = jnp.exp(-0.5 * pre_act * pre_act) * 0.3989422804014327
    return (pre_act * cdf_part, cdf_part + pre_act * density)


def gather_kernel(
    tensor, act, grad, bias, act_all, grad_all, bias_all, send, recv, fsend, frecv, own
):
    chips = tensor // 2
    me = lax.axis_index("tensor")
    sec = lax.axis_index("section")
    core = lax.rem(me, 2)
    chip = me // 2
    partner = chip * 2 + (1 - core)
    sources = (act, grad, bias)
    results = (act_all, grad_all, bias_all)

    def other(step):
        return lax.rem(chip + step, chips) * 2 + core

    def behind(step):
        return lax.rem(chip + chips - step, chips) * 2 + core

    barrier = pltpu.get_barrier_semaphore()
    for peer in [partner] + [other(step) for step in range(1, chips)]:
        pl.semaphore_signal(barrier, inc=1, device_id=(sec, peer), device_id_type=MESH)
    pl.semaphore_wait(barrier, chips)

    def far(kind, step):
        return pltpu.make_async_remote_copy(
            src_ref=sources[kind],
            dst_ref=results[kind].at[me],
            send_sem=send.at[kind, step],
            recv_sem=recv.at[kind, step],
            device_id=(sec, other(step)),
            device_id_type=MESH,
        )

    def near(kind, step):
        slot = behind(step)
        return pltpu.make_async_remote_copy(
            src_ref=sources[kind] if step == 0 else results[kind].at[slot],
            dst_ref=results[kind].at[slot],
            send_sem=fsend.at[kind, step],
            recv_sem=frecv.at[kind, step],
            device_id=(sec, partner),
            device_id_type=MESH,
        )

    everything = [(kind, step) for kind in (2, 0, 1) for step in range(1, chips)]
    if chips == 4:
        low_bit = lax.rem(chip, 2)
        side = chip + 1 - 2 * low_bit
        over = lax.rem(chip + 2, chips)
        across = lax.rem(side + 2, chips)

        def link(kind, step):
            return pltpu.make_async_remote_copy(
                src_ref=results[kind].at[(side, over)[kind] * 2 + core] if step == 3 else sources[kind],
                dst_ref=results[kind].at[((side, over)[kind] * 2 + core) if step == 3 else me],
                send_sem=send.at[kind, step],
                recv_sem=recv.at[kind, step],
                device_id=(sec, ((over, side)[kind] if step == 3 else (side, over)[step - 1]) * 2 + core),
                device_id_type=MESH,
            )

        def pass_on(kind, step):
            slot = (side, over, across)[step - 1] * 2 + core
            return pltpu.make_async_remote_copy(
                src_ref=results[kind].at[slot],
                dst_ref=results[kind].at[slot],
                send_sem=fsend.at[kind, step],
                recv_sem=frecv.at[kind, step],
                device_id=(sec, partner),
                device_id_type=MESH,
            )

        first = [(0, 1), (1, 2), (1, 1), (0, 2)]
        for kind, step in first:
            link(kind, step).start()
        for step in range(1, chips):
            far(2, step).start()
        for kind in (0, 1, 2):
            near(kind, 0).start()
            pltpu.make_async_copy(sources[kind], results[kind].at[me], own.at[kind]).start()
        for kind, step in first:
            link(kind, step).wait_recv()
            if step == kind + 1:
                link(kind, 3).start()
            pass_on(kind, step).start()
        for step in range(1, chips):
            far(2, step).wait_recv()
            near(2, step).start()
        for kind in (0, 1):
            link(kind, 3).wait_recv()
            pass_on(kind, 3).start()
        for kind in (0, 1):
            for step in range(1, chips):
                link(kind, step).wait_send()
                pass_on(kind, step).wait()
        for step in range(1, chips):
            far(2, step).wait_send()
            near(2, step).wait()
    else:
        for kind, step in everything:
            far(kind, step).start()
        for kind in (2, 0, 1):
            near(kind, 0).start()
            pltpu.make_async_copy(sources[kind], results[kind].at[me], own.at[kind]).start()
        for kind, step in everything:
            far(kind, step).wait_recv()
            near(kind, step).start()
        for kind, step in everything:
            far(kind, step).wait_send()
            near(kind, step).wait()
    for kind in (0, 1, 2):
        pltpu.make_async_copy(sources[kind], results[kind].at[me], own.at[kind]).wait()
        near(kind, 0).wait()


def tall(ref, cols, mask, row, slots):
    return jnp.concatenate(
        [
            jnp.where(
                mask[s, 0, row] > 0,
                ref[cols[s, 0, row]],
                jnp.zeros((BLK, BLK), BF16),
            )
            for s in range(slots)
        ],
        axis=0,
    )


def row_kernel(
    slots, group, dblocks, tensor,
    cols_in, mask_in, cols_out, mask_out, stored,
    w_in, w_out, act, grad, bias,
    hidden_out, low_out, part_out, bias_out,
    total, bias_wide,
):
    step = pl.program_id(0)
    hblocks = bias_wide.shape[0]

    @pl.when(step == 0)
    def _():
        total[...] = jnp.zeros_like(total)
        bias_out[...] = jnp.zeros_like(bias_out)
        bias_wide[...] = bias[...].reshape(hblocks, BLK).astype(F32)

    def wide(ref, g):
        return jnp.concatenate([ref[g, s] for s in range(slots)], axis=1)

    several = range(group)
    line = [step * group + g for g in several]
    where_row = [stored[0, line[g]] for g in several]
    pre_act = []
    for g in several:
        bias_row = bias_wide[pl.ds(where_row[g], 1), :]
        bias_col = jnp.transpose(jnp.broadcast_to(bias_row, (BLK, BLK)))
        pre_act.append(
            jnp.dot(
                wide(w_in, g), tall(act, cols_in, mask_in, line[g], slots), preferred_element_type=F32
            )
            + bias_col
        )
    grad_hidden = [
        jnp.dot(
            wide(w_out, g), tall(grad, cols_out, mask_out, line[g], slots), preferred_element_type=F32
        )
        for g in several
    ]
    turned = []
    for g in several:
        act_value, slope = gelu_parts(pre_act[g])
        hidden_out[g] = act_value.astype(BF16)
        grad_pre = grad_hidden[g] * slope
        low_out[g] = grad_pre.astype(BF16)
        turned.append(jnp.transpose(grad_pre))
    pieces = [
        jnp.dot(turned[g].astype(BF16), wide(w_in, g), preferred_element_type=F32) for g in several
    ]
    for g in several:
        bias_out[pl.ds(where_row[g], 1), :] = jnp.sum(turned[g], axis=0, keepdims=True)
        for s in range(slots):
            piece = pieces[g][:, s * BLK : (s + 1) * BLK]
            total[cols_in[s, 0, line[g]]] += jnp.where(mask_in[s, 0, line[g]] > 0, piece, 0.0)

    @pl.when(step == pl.num_programs(0) - 1)
    def _():
        chips = tensor // 2
        per = dblocks // tensor
        for chip in range(chips):
            for core in range(2):
                base = (chip * 2 + core) * per
                part_out[core, chip] = total[base : base + per].astype(BF16)


def scatter_kernel(
    tensor, sections, slots, rows, per, parts,
    cols_in, mask_in, cols_out, mask_out,
    part, bias_part, hidden, low, act, grad,
    tiles_in, tiles_out, bias_sum, handed,
    from_pair, pair_sum, from_chips, final, bias_from,
    pair_send, pair_recv, chip_send, chip_recv, bias_send, bias_recv, hand_send, hand_recv,
):
    chips = tensor // 2
    me = lax.axis_index("tensor")
    sec = lax.axis_index("section")
    core = lax.rem(me, 2)
    chip = me // 2
    partner = chip * 2 + (1 - core)
    before = lax.rem(sec + sections - 1, sections)
    after = lax.rem(sec + 1, sections)

    def ahead_chip(step):
        return lax.rem(chip + step, chips)

    barrier = pltpu.get_barrier_semaphore()
    for step in range(1, tensor):
        pl.semaphore_signal(
            barrier, inc=1, device_id=(sec, lax.rem(me + step, tensor)), device_id_type=MESH
        )
    for section in (before, after):
        pl.semaphore_signal(barrier, inc=1, device_id=(section, me), device_id_type=MESH)
    pl.semaphore_wait(barrier, tensor + 1)

    size = per // parts

    def pair(part_no):
        blocks = pl.ds(part_no * size, size)
        return pltpu.make_async_remote_copy(
            src_ref=part.at[1 - core, :, blocks],
            dst_ref=from_pair.at[:, blocks],
            send_sem=pair_send.at[part_no],
            recv_sem=pair_recv.at[part_no],
            device_id=(sec, partner),
            device_id_type=MESH,
        )

    for part_no in range(parts):
        pair(part_no).start()

    def bias_copy(step):
        peer = lax.rem(me + step, tensor)
        return pltpu.make_async_remote_copy(
            src_ref=bias_part.at[peer],
            dst_ref=bias_from.at[step],
            send_sem=bias_send.at[step],
            recv_sem=bias_recv.at[step],
            device_id=(sec, peer),
            device_id_type=MESH,
        )

    for step in range(1, tensor):
        bias_copy(step).start()

    def chip_copy(part_no, step):
        blocks = pl.ds(part_no * size, size)
        return pltpu.make_async_remote_copy(
            src_ref=pair_sum.at[step, blocks],
            dst_ref=from_chips.at[step, blocks],
            send_sem=chip_send.at[part_no, step],
            recv_sem=chip_recv.at[part_no, step],
            device_id=(sec, ahead_chip(step) * 2 + core),
            device_id_type=MESH,
        )

    def hand(part_no):
        blocks = pl.ds(part_no * size, size)
        return pltpu.make_async_remote_copy(
            src_ref=final.at[blocks],
            dst_ref=handed.at[blocks],
            send_sem=hand_send.at[part_no],
            recv_sem=hand_recv.at[part_no],
            device_id=(before, me),
            device_id_type=MESH,
        )

    def out_product(left, right):
        return lax.dot_general(
            left, right, (((1,), (1,)), ((), ())), preferred_element_type=F32
        ).astype(BF16)

    def one_row(row, carry):
        got_in = out_product(low[row], tall(act, cols_in, mask_in, row, slots))
        got_out = out_product(hidden[row], tall(grad, cols_out, mask_out, row, slots))
        for s in range(slots):
            tiles_in[row, s] = got_in[:, s * BLK : (s + 1) * BLK]
            tiles_out[row, s] = got_out[:, s * BLK : (s + 1) * BLK]
        return carry

    marks = [0]

    def compute_to(share):
        goal = (rows * share) // 32
        lax.fori_loop(marks[-1], goal, one_row, 0)
        marks.append(goal)

    for part_no in range(parts):
        compute_to((part_no + 1) * 4 // parts)
        pair(part_no).wait()
        mine = slice(part_no * size, (part_no + 1) * size)
        for step in list(range(1, chips)) + [0]:
            where_chip = ahead_chip(step)
            pair_sum[step, mine] = (
                part[core, where_chip, mine].astype(F32) + from_pair[where_chip, mine].astype(F32)
            ).astype(BF16)
            if step:
                chip_copy(part_no, step).start()

    for part_no in range(parts):
        compute_to(4 + (part_no + 1) * 24 // parts)
        mine = slice(part_no * size, (part_no + 1) * size)
        result = pair_sum[0, mine].astype(F32)
        for step in range(1, chips):
            chip_copy(part_no, step).wait()
            result = result + from_chips[step, mine].astype(F32)
        for block in range(size):
            final[part_no * size + block] = jnp.transpose(result[block]).astype(BF16)
        hand(part_no).start()

    compute_to(32)

    bias_total = bias_part[me]
    for step in range(1, tensor):
        bias_copy(step).wait()
        bias_total = bias_total + bias_from[step]
    bias_sum[...] = bias_total
    for part_no in range(parts):
        hand(part_no).wait()


def write_kernel(*refs):
    done = refs[8]
    copies = [pltpu.make_async_copy(refs[i], refs[4 + i], done.at[i]) for i in range(4)]
    for copy in copies:
        copy.start()
    for copy in copies:
        copy.wait()


def local(
    activations, out_grads, w_in, w_out, bias_in, cols_in, mask_in, cols_out, mask_out, block_rows
):
    tensor = lax.axis_size("tensor")
    sections = lax.axis_size("section")
    chips = tensor // 2
    _, rows, slots = cols_in.shape
    depth = activations.shape[1]
    per = depth // BLK
    dblocks = per * tensor
    hblocks = rows * tensor
    group = next(each for each in (8, 4, 1) if rows % each == 0)
    parts = 4 if per % 4 == 0 else 1
    tables = [jnp.transpose(each, (2, 0, 1)) for each in (cols_in, mask_in, cols_out, mask_out)]
    tables = [pltpu.with_memory_space_constraint(each, pltpu.HBM) for each in tables]
    block_rows = pltpu.with_memory_space_constraint(block_rows, pltpu.HBM)
    vmem_spec = pl.BlockSpec(memory_space=pltpu.VMEM)
    smem_spec = pl.BlockSpec(memory_space=pltpu.SMEM)
    dma = pltpu.SemaphoreType.DMA

    act_all, grad_all, bias_all = pl.pallas_call(
        functools.partial(gather_kernel, tensor),
        out_shape=(
            jax.ShapeDtypeStruct((tensor, per, BLK, BLK), BF16),
            jax.ShapeDtypeStruct((tensor, per, BLK, BLK), BF16),
            jax.ShapeDtypeStruct((tensor, rows, BLK), BF16),
        ),
        in_specs=[pl.BlockSpec(memory_space=pltpu.HBM)] * 3,
        out_specs=[vmem_spec] * 3,
        scratch_shapes=[dma((3, chips))] * 4 + [dma((3,))],
        compiler_params=pltpu.CompilerParams(
            collective_id=0, has_side_effects=True, vmem_limit_bytes=16 << 20
        ),
        name="gather_inputs",
    )(
        pltpu.with_memory_space_constraint(activations.reshape(per, BLK, BLK), pltpu.HBM),
        pltpu.with_memory_space_constraint(out_grads.reshape(per, BLK, BLK), pltpu.HBM),
        bias_in.reshape(rows, BLK),
    )
    act_all = act_all.reshape(dblocks, BLK, BLK)
    grad_all = grad_all.reshape(dblocks, BLK, BLK)

    def whole(*shape):
        return pl.BlockSpec(shape, lambda row, *_: (0,) * len(shape))

    tile_spec = pl.BlockSpec((group, slots, BLK, BLK), lambda row, *_: (row, 0, 0, 0))
    block_spec = pl.BlockSpec((group, BLK, BLK), lambda row, *_: (row, 0, 0))
    hidden, low, part, bias_part = pl.pallas_call(
        functools.partial(row_kernel, slots, group, dblocks, tensor),
        out_shape=(
            jax.ShapeDtypeStruct((rows, BLK, BLK), BF16),
            jax.ShapeDtypeStruct((rows, BLK, BLK), BF16),
            jax.ShapeDtypeStruct((2, chips, per, BLK, BLK), BF16),
            jax.ShapeDtypeStruct((hblocks, BLK), F32),
        ),
        grid_spec=pltpu.PrefetchScalarGridSpec(
            num_scalar_prefetch=5,
            grid=(rows // group,),
            in_specs=[
                tile_spec,
                tile_spec,
                whole(dblocks, BLK, BLK),
                whole(dblocks, BLK, BLK),
                whole(tensor, rows, BLK),
            ],
            out_specs=[
                block_spec,
                block_spec,
                whole(2, chips, per, BLK, BLK),
                whole(hblocks, BLK),
            ],
            scratch_shapes=[
                pltpu.VMEM((dblocks, BLK, BLK), F32),
                pltpu.VMEM((hblocks, BLK), F32),
            ],
        ),
        compiler_params=pltpu.CompilerParams(vmem_limit_bytes=42 << 20),
        name="rows",
    )(
        *tables, block_rows,
        w_in[0], w_out[0], act_all, grad_all, bias_all,
    )

    tiles_in, tiles_out, bias_sum, handed = pl.pallas_call(
        functools.partial(scatter_kernel, tensor, sections, slots, rows, per, parts),
        out_shape=(
            jax.ShapeDtypeStruct((rows, slots, BLK, BLK), BF16),
            jax.ShapeDtypeStruct((rows, slots, BLK, BLK), BF16),
            jax.ShapeDtypeStruct((rows, BLK), F32),
            jax.ShapeDtypeStruct((per, BLK, BLK), BF16),
        ),
        in_specs=[smem_spec] * 4 + [vmem_spec] * 6,
        out_specs=[vmem_spec] * 4,
        scratch_shapes=[
            pltpu.VMEM((chips, per, BLK, BLK), BF16),
            pltpu.VMEM((chips, per, BLK, BLK), BF16),
            pltpu.VMEM((chips, per, BLK, BLK), BF16),
            pltpu.VMEM((per, BLK, BLK), BF16),
            pltpu.VMEM((tensor, rows, BLK), F32),
            dma((parts,)), dma((parts,)),
            dma((parts, chips)), dma((parts, chips)),
            dma((tensor,)), dma((tensor,)),
            dma((parts,)), dma((parts,)),
        ],
        compiler_params=pltpu.CompilerParams(
            collective_id=1, has_side_effects=True, vmem_limit_bytes=16 << 20
        ),
        name="scatter_tiles",
    )(
        *tables,
        part, bias_part.reshape(tensor, rows, BLK), hidden, low, act_all, grad_all,
    )
    hbm_spec = pl.BlockSpec(memory_space=pl.ANY)
    tiles_in, tiles_out, bias_sum, handed = pl.pallas_call(
        write_kernel,
        out_shape=[
            jax.ShapeDtypeStruct(each.shape, each.dtype)
            for each in (tiles_in, tiles_out, bias_sum, handed)
        ],
        in_specs=[vmem_spec] * 4,
        out_specs=[hbm_spec] * 4,
        scratch_shapes=[dma((4,))],
        compiler_params=pltpu.CompilerParams(vmem_limit_bytes=16 << 20),
        name="write_results",
    )(tiles_in, tiles_out, bias_sum, handed)
    return (
        tiles_in[None],
        tiles_out[None],
        bias_sum.reshape(1, rows * BLK),
        handed.reshape(1, depth, BLK),
    )


def solution(mesh):
    return jax.shard_map(
        local,
        mesh=mesh,
        in_specs=(
            P("section", "tensor", None),
            P("section", "tensor", None),
            P("section", "tensor", None, None, None),
            P("section", "tensor", None, None, None),
            P("section", "tensor"),
            P("section", "tensor", None),
            P("section", "tensor", None),
            P("section", "tensor", None),
            P("section", "tensor", None),
            P("section", "tensor"),
        ),
        out_specs=(
            P("section", "tensor", None, None, None),
            P("section", "tensor", None, None, None),
            P("section", "tensor"),
            P("section", "tensor", None),
        ),
        check_vma=False,
    )
```
